32 devices in a mesh: groups: 2 (over y), vocab: 4 (over z), req: 4 (over x, core).
Axes of the slice: x: 2, y: 2, z: 4, core: 2. Of those that a mesh axis runs over, the one named last changes fastest.
Arguments:
- last_states: bfloat16 [512, 8192], P('groups', 'req'), parts along dimension 0, may hold values from -300 to 300
- head_weight: bfloat16 [8192, 32000], P('req', 'vocab'), may hold values from -1 to 1
- embed_table: bfloat16 [32000, 8192], P('vocab', 'req'), may hold values from -200 to 200
- norm_gain: bfloat16 [8192], P('req'), may hold values from 0.099609375 to 1.8984375
- qkv_weight: bfloat16 [8192, 10240], P('req', 'vocab'), may hold values from -0.0625 to 0.0625
- active: int32 [512], P('groups'), parts along dimension 0, may hold values 0 or 1
- slot_request: int32 [512], P('groups'), parts along dimension 0, may hold values from 0 to 255, each once
Outputs:
- soft_embed: bfloat16 [512, 8192], P('groups', 'req'), parts along dimension 0
- qkv_out: bfloat16 [512, 10240], P(('groups', 'req'), 'vocab'), parts along dimension 0
The draws below stay inside these ranges and needn't reach their ends.
There are 2 independent parts, one for each index of `groups`. The reference program is written for one: setup_inputs(seed, part) draws one part's arguments, and reference() takes and returns one part's arrays. A program takes and returns all parts, laid end to end along the dimension named above; an argument that names none is the same for every part. Nothing has to cross between parts.
Inputs may be any that keep to these rules, and one draw needn't show every extreme that they name: `slot_request`: each slot serves a different request.
All inputs are finite; a program needn't handle non-finite values.
Results may differ from the reference program's by a relative error of at most 0.006.
Values may be sent and summed in bfloat16 or wider, within the bound.
A program may use at most 192 MiB of HBM per device.

```python
import math
import jax
import jax.numpy as jnp
from jax import lax

D = 8192
V = 32000
QKV = 10240
ROWS = 256


def draw_last_states(key, part):
    subkeys = jax.random.split(key, 2)
    row_scale = jnp.exp(jax.random.uniform(subkeys[0], (ROWS, 1), minval=math.log(18.0), maxval=math.log(48.0)))
    base = jnp.clip(jax.random.normal(subkeys[1], (ROWS, D)), -6.0, 6.0) * row_scale
    return base.astype(jnp.float32).astype(jnp.bfloat16)


def draw_head_weight(key, part):
    column = jnp.arange(V, dtype=jnp.float32)[None, :] / V
    index = jnp.arange(V)[None, :]
    rare = index >= V - V // 16
    factor = jnp.where(rare, 0.85, 0.6 + 0.8 * column)
    base = jnp.clip(jax.random.normal(key, (D, V)), -6.0, 6.0) * factor * 0.12 / math.sqrt(D)
    return base.astype(jnp.float32).astype(jnp.bfloat16)


def draw_embed_table(key, part):
    subkeys = jax.random.split(key, 5)
    row_scale = jnp.exp(jax.random.uniform(subkeys[0], (V, 1), minval=0.0, maxval=math.log(10.0)))
    position = jnp.arange(D, dtype=jnp.float32)[None, :] / D
    rare = jnp.arange(V)[:, None] >= V - V // 16
    col_scale = jnp.exp(jax.random.uniform(subkeys[1], (1, D), minval=0.0, maxval=math.log(10.0))) * 3.0 ** (0.5 * position)
    bulk = jnp.clip(jax.random.normal(subkeys[2], (V, D)), -6.0, 6.0) * row_scale * col_scale
    heavy = 60.0 * jnp.clip(jax.random.normal(subkeys[4], (V, D)), -3.2, 3.2)
    base = jnp.where(rare, heavy, 0.05 * bulk)
    return base.astype(jnp.float32).astype(jnp.bfloat16)


def place_ends(entries, key, smallest, high):
    extent = entries.shape
    place = [jax.random.randint(jax.random.fold_in(key, axis), (), 0, extent[axis]) for axis in range(len(extent))]
    entries = entries.at[tuple(place)].set(smallest)
    longest = extent.index(max(extent))
    place[longest] = (place[longest] + 1) % extent[longest]
    return entries.at[tuple(place)].set(high)


def block_levels(own_key, dims, cuts, least, high):
    loudness, own = 1.0, jax.random.fold_in(own_key, 6)
    for axis_at, blocks in cuts:
        steps = jnp.exp(jax.random.uniform(jax.random.fold_in(own, axis_at), (blocks,), jnp.float32, least / len(cuts), high / len(cuts)))
        loudness = loudness * jnp.repeat(steps, dims[axis_at] // blocks).reshape([-1 if axis == axis_at else 1 for axis in range(len(dims))])
    return loudness


def normal_values(own_key, dims, scale, bound, pieces=(), kind=jnp.bfloat16):
    level = block_levels(own_key, dims, pieces, -0.22, 0.18) if pieces else 1.0
    drawn = jax.random.normal(own_key, dims, jnp.float32) * scale * level
    return jnp.minimum(jnp.maximum(drawn, -bound), bound).astype(kind)


def setup_inputs(seed: int = 0, part: int = 0) -> dict:
    splits = jax.random.split(jax.random.key(seed), 8)
    part_splits = jax.random.split(jax.random.fold_in(splits[7], part), 8)
    last_states = draw_last_states(jax.random.fold_in(jax.random.fold_in(splits[7], part), 71), part)
    head_weight = draw_head_weight(jax.random.fold_in(splits[7], 71), part)
    embed_table = draw_embed_table(jax.random.fold_in(splits[7], 71), part)
    norm_gain = jnp.clip(1.0 + 0.18 * jax.random.normal(splits[3], (D,), jnp.float32), 0.099609375, 1.8984375).astype(jnp.bfloat16)
    qkv_weight = normal_values(splits[4], (D, QKV), D ** -0.5, 0.0625, ((0, 4), (1, 4)))
    active = place_ends((jax.random.randint(part_splits[5], (ROWS,), 0, 4) < 3).astype(jnp.int32), jax.random.fold_in(part_splits[5], 1), 0, 1)
    slot_request = jax.random.permutation(part_splits[6], ROWS).astype(jnp.int32)
    return dict(last_states=last_states, head_weight=head_weight, embed_table=embed_table, norm_gain=norm_gain, qkv_weight=qkv_weight, active=active, slot_request=slot_request)


def reference(last_states, head_weight, embed_table, norm_gain, qkv_weight, active, slot_request):
    slot_states = jnp.take(last_states, slot_request.astype(jnp.int32), axis=0)
    logits = jnp.dot(slot_states, head_weight, preferred_element_type=jnp.float32)
    row_top = lax.optimization_barrier(jnp.max(logits, axis=1, keepdims=True))
    shifted = jnp.exp(logits - row_top)
    row_total = lax.optimization_barrier(jnp.sum(shifted, axis=1, keepdims=True))
    weights = (shifted / row_total * active.astype(jnp.float32)[:, None]).astype(jnp.bfloat16)
    mixed = jnp.dot(weights, embed_table, preferred_element_type=jnp.float32)
    soft_embed = lax.optimization_barrier(mixed.astype(jnp.bfloat16))
    widened = soft_embed.astype(jnp.float32)
    inv_rms = lax.rsqrt(lax.optimization_barrier(jnp.mean(widened * widened, axis=1, keepdims=True)) + 1e-05)
    normed = (widened * inv_rms * norm_gain.astype(jnp.float32)[None, :]).astype(jnp.bfloat16)
    qkv_out = jnp.dot(normed, qkv_weight, preferred_element_type=jnp.float32).astype(jnp.bfloat16)
    return (soft_embed, qkv_out)
```

```python
import functools

import jax
import jax.numpy as jnp
from jax import lax
from jax.experimental import pallas as pl
from jax.experimental.pallas import tpu as pltpu
from jax.sharding import PartitionSpec as P

MESH = pl.DeviceIdType.MESH
VMEM_LIMIT = 63 * 1024 * 1024
RING = 4
AHEAD = 3
LEVELS = 65535.0


def greet(targets):
    barrier = pltpu.get_barrier_semaphore()
    for target in targets:
        pl.semaphore_signal(barrier, inc=1, device_id=target, device_id_type=MESH)
    pl.semaphore_wait(barrier, len(targets))


def remote(src, dst, send, recv, target):
    return pltpu.make_async_remote_copy(
        src_ref=src, dst_ref=dst, send_sem=send, recv_sem=recv, device_id=target, device_id_type=MESH
    )


def round_up(n, m):
    return (n + m - 1) // m * m


def column_chunks(words, chunk):
    whole = words // chunk * chunk
    rest = words - whole
    chunks = [(i * chunk, chunk) for i in range(words // chunk)]
    half = chunk // 2
    if rest > half:
        chunks = [(whole + half, rest - half), (whole, half)] + chunks
    elif rest:
        chunks = [(whole, rest)] + chunks
    return chunks


class Plan:
    def __init__(self, rows, width, words, columns, nx, nz):
        self.rows, self.width, self.words, self.columns = rows, width, words, columns
        self.nx, self.nz = nx, nz
        steps = 4
        while steps > 1 and (rows // steps // nz) % 16:
            steps //= 2
        self.steps = steps
        self.own_rows = rows // (2 * nx)
        self.s = self.own_rows // steps
        self.block = 2 * nx * self.s
        self.hb = self.block // 2
        self.hp = self.hb // 2
        self.piece = self.block // nz
        self.chunk = min(1024, width)
        self.chunks = column_chunks(words, self.chunk)
        self.halves = 2
        self.qtile = next(t for t in (640, 512, 256, 128) if columns % t == 0)
        self.qwide = columns + 128


def kernel_body(p, states_ref, head_ref, embed_ref, gain_ref, qkv_ref, active_ref, slot_ref,
                soft_ref, out_ref,
                table, part, ring_out, ring_in, code_out, code_in, scale_out, scale_in,
                weights, stats, act_slot, act_block, hot_slot, hot, mixed, inbox, scaled, qbuf,
                q_all, q_recv, q_out, q_in,
                state_sem, head_sem, embed_sem, q_sem, ring_send, ring_recv, code_send, code_recv,
                scale_send, scale_recv, stat_send, stat_recv, pair_send, pair_recv,
                mix_send, mix_recv, soft_send, soft_recv, qp_send, qp_recv, qx_send, qx_recv):
    nx, nz, steps, s, hb, hp = p.nx, p.nz, p.steps, p.s, p.hb, p.hp
    rows, width, words, own_rows, block, piece = p.rows, p.width, p.words, p.own_rows, p.block, p.piece
    me = lax.axis_index("req")
    z = lax.axis_index("vocab")
    chip, core = lax.div(me, 2), lax.rem(me, 2)
    mate = chip * 2 + (1 - core)
    partner = {"req": mate}

    def chip_at(d):
        return lax.rem(chip + d, nx)

    def peer(d):
        return {"req": chip_at(d) * 2 + core}

    def z_at(d):
        return lax.rem(z + d, nz)

    state_copy = pltpu.make_async_copy(states_ref, mixed, state_sem)
    state_copy.start()
    nk = len(p.chunks)

    def words_of(ref, k):
        start, size = p.chunks[k]
        return ref.at[pl.ds(start, size), :]

    head_copies = [pltpu.make_async_copy(words_of(head_ref, k), words_of(table, k), head_sem.at[k]) for k in range(nk)]
    embed_copies = [pltpu.make_async_copy(words_of(embed_ref, k), words_of(table, k), embed_sem.at[k])
                    for k in range(nk)]
    for k in range(min(nk, AHEAD)):
        head_copies[k].start()

    nt = p.columns // p.qtile

    def q_load(g):
        return pltpu.make_async_copy(
            qkv_ref.at[:, pl.ds(g % nt * p.qtile, p.qtile)], qbuf.at[g % 2], q_sem.at[g % 2])

    request = slot_ref[...].reshape(1, rows)
    choose = (lax.broadcasted_iota(jnp.int32, (rows, rows), 0) == request).astype(jnp.float32)
    hot_slot[...] = choose.T.astype(hot_slot.dtype)
    live = jnp.broadcast_to(active_ref[...].reshape(1, rows).astype(jnp.float32), (128, rows))
    act_slot[...] = live.T
    for h in range(2):
        side = core if h == 0 else 1 - core
        for j in range(steps):
            for o in range(nx):
                to = h * (steps * hb) + j * hb + o * s
                at = pl.multiple_of((side * nx + o) * own_rows + j * s, s)
                hot[to : to + s, :] = hot_slot[pl.ds(at, s), :]
    for j in range(steps):
        for o in range(2 * nx):
            act_block[j, o * s : (o + 1) * s, :] = act_slot[o * own_rows + j * s : o * own_rows + (j + 1) * s, :]
    state_copy.wait()
    wide_tile = min(512, width)

    @pl.loop(0, width // wide_tile)
    def _(c):
        columns = pl.ds(pl.multiple_of(c * wide_tile, wide_tile), wide_tile)
        soft_ref[:, columns] = jnp.dot(
            hot[...], mixed[:, columns], preferred_element_type=jnp.float32
        ).astype(soft_ref.dtype)

    greet([partner] + [peer(d) for d in range(1, nx)]
          + [{"vocab": z_at(d)} for d in range(1, nz)]
          + [{"vocab": z_at(d), "req": mate} for d in range(1, nz)])

    half_rows = steps * hb
    ring_copies, code_copies, scale_copies = {}, {}, {}
    lane = lax.broadcasted_iota(jnp.int32, (hb, 128), 1)

    def logits(k):
        start, size = p.chunks[k]
        slot = k % RING
        head_copies[k].wait()
        if k >= RING:
            ring_copies[k - RING].wait_send()

        def tile(at, count):
            res = lax.dot_general(soft_ref[...], table[pl.ds(start + at, count), :], (((1,), (1,)), ((), ())),
                                  preferred_element_type=jnp.float32)
            part[:, pl.ds(start + at, count)] = res[:half_rows]
            ring_out[slot, :, pl.ds(at, count)] = res[half_rows:]

        t = 512
        if size % t or size <= t:
            tile(0, size)
        else:
            pl.loop(0, size // t)(lambda c: tile(pl.multiple_of(c * t, t), t))
        span = pl.ds(0, round_up(size, 128))
        copy = remote(ring_out.at[slot, :, span], ring_in.at[slot, :, span],
                      ring_send.at[slot], ring_recv.at[slot], partner)
        copy.start()
        ring_copies[k] = copy

    def encode(k):
        start, size = p.chunks[k]
        slot = k % RING
        ring_copies[k].wait_recv()
        for j in range(steps):
            mine = slice(j * hb, (j + 1) * hb)
            v = part[mine, start : start + size] + ring_in[slot, mine, 0:size]
            part[mine, start : start + size] = v
            low = jnp.min(v, axis=1, keepdims=True)
            step = jnp.maximum((jnp.max(v, axis=1, keepdims=True) - low) / LEVELS, 1e-30)
            level = ((v - low) * (1.0 / step) + 0.5).astype(jnp.int32)
            code_out[j, :, start : start + size] = level[:hp] | (level[hp:] << 16)
            pair = jnp.where(lane == 2 * k, low, step)
            scale_out[j] = pair if k == 0 else jnp.where(lane < 2 * k, scale_out[j], pair)
            if j == 0:
                send_codes(0, k)

    def send_codes(j, k):
        start, size = (0, words) if k is None else p.chunks[k]
        index = nk + j if k is None else k
        span = pl.ds(start, size)
        for d in range(1, nx):
            copy = remote(code_out.at[j, :, span], code_in.at[d - 1, j, :, span],
                          code_send.at[d - 1, index], code_recv.at[d - 1, index], peer(d))
            copy.start()
            code_copies[d, j, k] = copy

    def send_scales(j):
        for d in range(1, nx):
            copy = remote(scale_out.at[j], scale_in.at[d - 1, j], scale_send.at[d - 1, j],
                          scale_recv.at[d - 1, j], peer(d))
            copy.start()
            scale_copies[d, j] = copy

    loaded = 0
    for k in range(nk):
        logits(k)
        if k + AHEAD < nk:
            head_copies[k + AHEAD].start()
        else:
            while loaded <= k:
                embed_copies[loaded].start()
                loaded += 1
        if k > 0:
            encode(k - 1)
    encode(nk - 1)
    send_scales(0)
    for j in range(1, steps):
        send_codes(j, None)
        send_scales(j)
    q_load(0).start()
    if steps * nt > 1:
        q_load(1).start()

    stat_copies, pair_copies, mix_copies, soft_copies, qp_copies, qx_copies = {}, {}, {}, {}, {}, {}

    def half_of(j):
        return pl.ds(pl.multiple_of(core * hb, hb), hb)

    def softmax(j):
        mine = slice(j * hb, (j + 1) * hb)
        for d in range(1, nx):
            if j > 0:
                code_copies[d, j, None].wait_recv()
            scale_copies[d, j].wait_recv()
        top = None
        for k, (start, size) in enumerate(p.chunks):
            span = slice(start, start + size)
            upper, lower = part[mine, span][:hp], part[mine, span][hp:]
            for d in range(1, nx):
                if j == 0:
                    code_copies[d, j, k].wait_recv()
                word = code_in[d - 1, j, :, span]
                low = scale_in[d - 1, j][:, 2 * k : 2 * k + 1]
                step = scale_in[d - 1, j][:, 2 * k + 1 : 2 * k + 2]
                upper = upper + ((word & 65535).astype(jnp.float32) * step[:hp] + low[:hp])
                lower = lower + (((word >> 16) & 65535).astype(jnp.float32) * step[hp:] + low[hp:])
            part[j * hb : j * hb + hp, span] = upper
            part[j * hb + hp : (j + 1) * hb, span] = lower
            highest = jnp.concatenate(
                [jnp.max(upper, axis=1, keepdims=True), jnp.max(lower, axis=1, keepdims=True)], axis=0)
            top = highest if top is None else jnp.maximum(top, highest)
        total = jnp.zeros_like(top)
        for start, size in p.chunks:
            span = slice(start, start + size)
            e = jnp.exp(part[mine, span] - top)
            weights[j, half_of(j), span] = e.astype(weights.dtype)
            total = total + jnp.sum(e, axis=1, keepdims=True)
        stats[j, z, half_of(j), :] = jnp.where(lane < 64, top, total)
        block_rows = weights.at[j, half_of(j), :]
        copy = remote(block_rows, block_rows, pair_send.at[j], pair_recv.at[j], partner)
        copy.start()
        pair_copies[j] = copy
        for d in range(nz):
            for r in range(2):
                if d == 0 and r == 0:
                    continue
                target = {"req": mate} if r else {}
                if d:
                    target["vocab"] = z_at(d)
                rowset = stats.at[j, z, half_of(j), :]
                copy = remote(rowset, rowset, stat_send.at[j, d, r], stat_recv.at[j, d, r], target)
                copy.start()
                stat_copies[j, d, r] = copy

    half = width // p.halves
    tile = min(512, half)

    def piece_of(j, owner):
        return pl.ds(pl.multiple_of(j * block + owner * piece, piece), piece)

    def mix(j):
        if j == 0:
            for copy in embed_copies:
                copy.wait()
        pair_copies[j].wait_recv()
        for d in range(nz):
            for r in range(2):
                if d or r:
                    stat_copies[j, d, r].wait_recv()
        row_top = stats[j, 0][:, 0:1]
        for i in range(1, nz):
            row_top = jnp.maximum(row_top, stats[j, i][:, 0:1])
        row_total = jnp.zeros_like(row_top)
        for i in range(nz):
            other = stats[j, i]
            row_total = row_total + other[:, 64:65] * jnp.exp(other[:, 0:1] - row_top)
        factor = jnp.exp(stats[j, z][:, 0:1] - row_top) / row_total * act_block[j][:, 0:1]
        for h in range(p.halves):

            @pl.loop(h * half // tile, (h + 1) * half // tile)
            def _(c):
                columns = pl.ds(pl.multiple_of(c * tile, tile), tile)
                mixed[j * block : (j + 1) * block, columns] = (jnp.dot(
                    weights[j], table[:, columns], preferred_element_type=jnp.float32
                ) * factor).astype(mixed.dtype)

            columns = pl.ds(h * half, half)
            for d in range(1, nz):
                copy = remote(mixed.at[piece_of(j, z_at(d)), columns], inbox.at[j, d - 1, :, columns],
                              mix_send.at[j, h, d - 1], mix_recv.at[j, h, d - 1], {"vocab": z_at(d)})
                copy.start()
                mix_copies[j, h, d] = copy

    unit = min(s, piece)

    def collect(j):
        for h in range(p.halves):
            columns = pl.ds(h * half, half)
            total = mixed[piece_of(j, z), columns].astype(jnp.float32)
            for d in range(1, nz):
                mix_copies[j, h, d].wait_recv()
                total = total + inbox[j, d - 1, :, columns].astype(jnp.float32)
            total = total.astype(soft_ref.dtype)
            for u in range(piece // unit):
                at = z * piece + u * unit
                slot = lax.div(at, s) * own_rows + j * s + lax.rem(at, s)
                place = soft_ref.at[pl.ds(pl.multiple_of(slot, unit), unit), columns]
                place[...] = total[u * unit : (u + 1) * unit]
                for d in range(1, nz):
                    copy = remote(place, place, soft_send.at[j, h, u, d - 1],
                                  soft_recv.at[j, h, u, d - 1], {"vocab": z_at(d)})
                    copy.start()
                    soft_copies[j, h, u, d] = copy

    gain = gain_ref[...].reshape(1, width).astype(jnp.float32)

    def project(j):
        for h in range(p.halves):
            for u in range(piece // unit):
                for d in range(1, nz):
                    soft_copies[j, h, u, d].wait_recv()
        for side in range(2):
            for c in range(nx):
                owner = c * 2 + side
                v = soft_ref[owner * own_rows + j * s : owner * own_rows + (j + 1) * s, :].astype(jnp.float32)
                square = jnp.sum(v * v, axis=1, keepdims=True)
                q_all[j, side, c * s : (c + 1) * s, p.columns :] = jnp.broadcast_to(square, (s, 128))
                at = side * hb + c * s
                scaled[at : at + s, :] = (v * gain).astype(scaled.dtype)
        for i in range(nt):
            g = j * nt + i
            q_load(g).wait()
            res = jnp.dot(scaled[...], qbuf[g % 2], preferred_element_type=jnp.float32)
            span = slice(i * p.qtile, (i + 1) * p.qtile)
            q_all[j, 0, :, span] = res[:hb]
            q_all[j, 1, :, span] = res[hb:]
            if g + 2 < steps * nt:
                q_load(g + 2).start()
        copy = remote(q_all.at[j, 1 - core], q_recv.at[j], qp_send.at[j], qp_recv.at[j], partner)
        copy.start()
        qp_copies[j] = copy

    lane_s = lax.broadcasted_iota(jnp.int32, (s, 128), 1)

    def swap(j):
        qp_copies[j].wait_recv()
        for d in range(1, nx):
            at = pl.ds(pl.multiple_of(chip_at(d) * s, s), s)
            v = q_all[j, core, at, :] + q_recv[j, at, :]
            q_out[j, d - 1, :, : p.columns] = v[:, : p.columns].astype(q_out.dtype)
            square = v[:, p.columns :]
            high = square.astype(q_out.dtype).astype(jnp.float32)
            q_out[j, d - 1, :, p.columns :] = jnp.where(lane_s < 64, high, square - high).astype(q_out.dtype)
            copy = remote(q_out.at[j, d - 1], q_in.at[j, d - 1], qx_send.at[j, d - 1],
                          qx_recv.at[j, d - 1], peer(d))
            copy.start()
            qx_copies[j, d] = copy

    def finish(j):
        at = pl.ds(pl.multiple_of(chip * s, s), s)
        v = q_all[j, core, at, :] + q_recv[j, at, :]
        square = v[:, p.columns : p.columns + 1]
        v = v[:, : p.columns]
        for d in range(1, nx):
            qx_copies[j, d].wait_recv()
            v = v + q_in[j, d - 1, :, : p.columns].astype(jnp.float32)
            sent = q_in[j, d - 1, :, p.columns :].astype(jnp.float32)
            square = square + (sent[:, 0:1] + sent[:, 64:65])
        inv_rms = lax.rsqrt(square / (width * 2 * nx) + 1e-05)
        out_ref[j * s : (j + 1) * s, :] = (v * inv_rms).astype(out_ref.dtype)

    for t in range(steps):
        softmax(t)
        if t >= 1:
            collect(t - 1)
        mix(t)
        if t >= 1:
            project(t - 1)
    for t in range(steps - 1):
        swap(t)
    collect(steps - 1)
    for t in range(steps - 1):
        finish(t)
    project(steps - 1)
    swap(steps - 1)
    finish(steps - 1)

    for k in range(max(0, nk - RING), nk):
        ring_copies[k].wait_send()
    for group in (code_copies, scale_copies, stat_copies, pair_copies, mix_copies, soft_copies, qp_copies,
                  qx_copies):
        for copy in group.values():
            copy.wait_send()


def on_device(nx, nz, last_states, head_weight, embed_table, norm_gain, qkv_weight, active, slot_request):
    rows, width = last_states.shape
    p = Plan(rows, width, head_weight.shape[1], qkv_weight.shape[1], nx, nz)
    steps, s, hb, hp, block, piece = p.steps, p.s, p.hb, p.hp, p.block, p.piece
    words, nk, far = p.words, len(p.chunks), max(nx - 1, 1)
    units = piece // min(s, piece)
    dma, vmem, f32, bf16 = pltpu.SemaphoreType.DMA, pltpu.VMEM, jnp.float32, jnp.bfloat16
    anywhere, inside = pl.BlockSpec(memory_space=pl.ANY), pl.BlockSpec(memory_space=pltpu.VMEM)
    return pl.pallas_call(
        functools.partial(kernel_body, p),
        out_shape=(jax.ShapeDtypeStruct((rows, width), bf16), jax.ShapeDtypeStruct((p.own_rows, p.columns), bf16)),
        in_specs=[anywhere, anywhere, anywhere, inside, anywhere, inside, inside],
        out_specs=(inside, inside),
        scratch_shapes=[
            vmem((words, width), bf16),
            vmem((steps * hb, words), f32),
            vmem((RING, steps * hb, p.chunk), f32),
            vmem((RING, steps * hb, p.chunk), f32),
            vmem((steps, hp, words), jnp.int32),
            vmem((far, steps, hp, words), jnp.int32),
            vmem((steps, hb, 128), f32),
            vmem((far, steps, hb, 128), f32),
            vmem((steps, block, words), bf16),
            vmem((steps, nz, block, 128), f32),
            vmem((rows, 128), f32),
            vmem((steps, block, 128), f32),
            vmem((rows, rows), bf16),
            vmem((rows, rows), bf16),
            vmem((rows, width), bf16),
            vmem((steps, nz - 1, piece, width), bf16),
            vmem((block, width), bf16),
            vmem((2, width, p.qtile), bf16),
            vmem((steps, 2, hb, p.qwide), f32),
            vmem((steps, hb, p.qwide), f32),
            vmem((steps, far, s, p.qwide), bf16),
            vmem((steps, far, s, p.qwide), bf16),
            dma, dma((nk,)), dma((nk,)), dma((2,)),
            dma((RING,)), dma((RING,)),
            dma((far, nk + steps)), dma((far, nk + steps)),
            dma((far, steps)), dma((far, steps)),
            dma((steps, nz, 2)), dma((steps, nz, 2)),
            dma((steps,)), dma((steps,)),
            dma((steps, p.halves, nz - 1)), dma((steps, p.halves, nz - 1)),
            dma((steps, p.halves, units, nz - 1)), dma((steps, p.halves, units, nz - 1)),
            dma((steps,)), dma((steps,)),
            dma((steps, far)), dma((steps, far)),
        ],
        compiler_params=pltpu.CompilerParams(
            collective_id=0, has_side_effects=True, vmem_limit_bytes=VMEM_LIMIT
        ),
        name="decode_step",
    )(last_states, head_weight.T, embed_table, norm_gain, qkv_weight, active, slot_request)


def solution(mesh):
    nx, nz = mesh.shape["req"] // 2, mesh.shape["vocab"]
    return jax.shard_map(
        functools.partial(on_device, nx, nz),
        mesh=mesh,
        in_specs=(
            P("groups", "req"),
            P("req", "vocab"),
            P("vocab", "req"),
            P("req"),
            P("req", "vocab"),
            P("groups"),
            P("groups"),
        ),
        out_specs=(P("groups", "req"), P(("groups", "req"), "vocab")),
        check_vma=False,
    )
```

```python
import functools

import jax
import jax.numpy as jnp
from jax import lax
from jax.experimental import pallas as pl
from jax.experimental.pallas import tpu as pltpu
from jax.sharding import PartitionSpec as P

MESH = pl.DeviceIdType.MESH
VMEM_LIMIT = 63 * 1024 * 1024
RING = 4
EARLY = 4
AHEAD = 2
LEVELS = 65535.0


def remote(src, dst, send, recv, target):
    return pltpu.make_async_remote_copy(
        src_ref=src, dst_ref=dst, send_sem=send, recv_sem=recv, device_id=target, device_id_type=MESH
    )


def round_up(n, m):
    return (n + m - 1) // m * m


def column_chunks(words, chunk):
    whole = words // chunk * chunk
    rest = words - whole
    chunks = [(i * chunk, chunk) for i in range(words // chunk)]
    half = chunk // 2
    if rest > half:
        chunks = [(whole + half, rest - half), (whole, half)] + chunks
    elif rest:
        chunks = [(whole, rest)] + chunks
    return chunks


class Plan:
    def __init__(self, rows, width, words, columns, nx, nz):
        self.rows, self.width, self.words, self.columns = rows, width, words, columns
        self.nx, self.nz = nx, nz
        steps = 4
        while steps > 1 and (rows // steps // nz) % 16:
            steps //= 2
        self.steps = steps
        self.own_rows = rows // (2 * nx)
        self.s = self.own_rows // steps
        self.block = 2 * nx * self.s
        self.hb = self.block // 2
        self.hp = self.hb // 2
        self.piece = self.block // nz
        self.chunk = min(768, width)
        self.chunks = column_chunks(words, self.chunk)
        self.halves = 2
        self.qtile = next(t for t in (512, 640, 256, 128) if columns % t == 0)
        self.qwide = columns + 128


def kernel_body(p, states_ref, head_ref, embed_ref, gain_ref, qkv_ref, active_ref, slot_ref,
                soft_ref, out_ref,
                table, part, ring_out, ring_in, code_out, code_in, scale_out, scale_in,
                weights, stats, act_slot, act_block, hot_slot, hot, mixed, inbox, scaled, qbuf,
                q_all, q_recv, q_out, q_in,
                state_sem, head_sem, embed_sem, q_sem, ring_send, ring_recv, code_send, code_recv,
                scale_send, scale_recv, stat_send, stat_recv, pair_send, pair_recv,
                mix_send, mix_recv, soft_send, soft_recv, qp_send, qp_recv, qx_send, qx_recv):
    nx, nz, steps, s, hb, hp = p.nx, p.nz, p.steps, p.s, p.hb, p.hp
    rows, width, words, own_rows, block, piece = p.rows, p.width, p.words, p.own_rows, p.block, p.piece
    me = lax.axis_index("req")
    z = lax.axis_index("vocab")
    chip, core = lax.div(me, 2), lax.rem(me, 2)
    mate = chip * 2 + (1 - core)
    partner = {"req": mate}

    def chip_at(d):
        return lax.rem(chip + d, nx)

    def peer(d):
        return {"req": chip_at(d) * 2 + core}

    def z_at(d):
        return lax.rem(z + d, nz)

    barrier = pltpu.get_barrier_semaphore()
    friends = ([partner] + [peer(d) for d in range(1, nx)]
               + [{"vocab": z_at(d)} for d in range(1, nz)]
               + [{"vocab": z_at(d), "req": mate} for d in range(1, nz)])
    for friend in friends:
        pl.semaphore_signal(barrier, inc=1, device_id=friend, device_id_type=MESH)

    state_copy = pltpu.make_async_copy(states_ref, mixed, state_sem)
    state_copy.start()
    nk = len(p.chunks)

    def words_of(ref, k):
        start, size = p.chunks[k]
        return ref.at[pl.ds(start, size), :]

    head_copies = [pltpu.make_async_copy(words_of(head_ref, k), words_of(table, k), head_sem.at[k]) for k in range(nk)]
    embed_copies = [pltpu.make_async_copy(words_of(embed_ref, k), words_of(table, k), embed_sem.at[k])
                    for k in range(nk)]
    for k in range(min(nk, AHEAD)):
        head_copies[k].start()

    nt = p.columns // p.qtile

    def q_load(g):
        return pltpu.make_async_copy(
            qkv_ref.at[:, pl.ds(g % nt * p.qtile, p.qtile)], qbuf.at[g % 2], q_sem.at[g % 2])

    request = slot_ref[...].reshape(1, rows)
    choose = (lax.broadcasted_iota(jnp.int32, (rows, rows), 0) == request).astype(jnp.float32)
    hot_slot[...] = choose.T.astype(hot_slot.dtype)
    live = jnp.broadcast_to(active_ref[...].reshape(1, rows).astype(jnp.float32), (128, rows))
    act_slot[...] = live.T
    for h in range(2):
        side = core if h == 0 else 1 - core
        for j in range(steps):
            for o in range(nx):
                to = h * (steps * hb) + j * hb + o * s
                at = pl.multiple_of((side * nx + o) * own_rows + j * s, s)
                hot[to : to + s, :] = hot_slot[pl.ds(at, s), :]
    for j in range(steps):
        for o in range(2 * nx):
            act_block[j, o * s : (o + 1) * s, :] = act_slot[o * own_rows + j * s : o * own_rows + (j + 1) * s, :]
    state_copy.wait()
    wide_tile = min(512, width)

    @pl.loop(0, width // wide_tile)
    def _(c):
        columns = pl.ds(pl.multiple_of(c * wide_tile, wide_tile), wide_tile)
        soft_ref[:, columns] = jnp.dot(
            hot[...], mixed[:, columns], preferred_element_type=jnp.float32
        ).astype(soft_ref.dtype)

    half_rows = steps * hb
    ring_copies, code_copies, scale_copies = {}, {}, {}
    lane = lax.broadcasted_iota(jnp.int32, (hb, 128), 1)

    def logits(k):
        start, size = p.chunks[k]
        slot = k % RING
        head_copies[k].wait()
        if k + AHEAD < nk:
            head_copies[k + AHEAD].start()
        if k >= RING:
            ring_copies[k - RING].wait_send()

        def tile(at, count):
            res = lax.dot_general(soft_ref[...], table[pl.ds(start + at, count), :], (((1,), (1,)), ((), ())),
                                  preferred_element_type=jnp.float32)
            part[:, pl.ds(start + at, count)] = res[:half_rows]
            ring_out[slot, :, pl.ds(at, count)] = res[half_rows:]

        tile(0, size)

    def ship(k):
        size, slot = p.chunks[k][1], k % RING
        span = pl.ds(0, round_up(size, 128))
        copy = remote(ring_out.at[slot, :, span], ring_in.at[slot, :, span],
                      ring_send.at[slot], ring_recv.at[slot], partner)
        copy.start()
        ring_copies[k] = copy

    def encode(k):
        start, size = p.chunks[k]
        slot = k % RING
        ring_copies[k].wait_recv()
        for j in range(steps):
            mine = slice(j * hb, (j + 1) * hb)
            v = part[mine, start : start + size] + ring_in[slot, mine, 0:size]
            part[mine, start : start + size] = v
            low = jnp.min(v, axis=1, keepdims=True)
            step = jnp.maximum((jnp.max(v, axis=1, keepdims=True) - low) / LEVELS, 1e-30)
            level = ((v - low) * (1.0 / step) + 0.5).astype(jnp.int32)
            code_out[j, :, start : start + size] = level[:hp] | (level[hp:] << 16)
            pair = jnp.where(lane == 2 * k, low, step)
            scale_out[j] = pair if k == 0 else jnp.where(lane < 2 * k, scale_out[j], pair)
            if j == 0:
                send_codes(0, k)

    def send_codes(j, k):
        start, size = (0, words) if k is None else p.chunks[k]
        size = round_up(size, 128)
        index = nk + j if k is None else k
        span = pl.ds(start, size)
        for d in range(1, nx):
            copy = remote(code_out.at[j, :, span], code_in.at[d - 1, j, :, span],
                          code_send.at[d - 1, index], code_recv.at[d - 1, index], peer(d))
            copy.start()
            code_copies[d, j, k] = copy

    def send_scales(j):
        for d in range(1, nx):
            copy = remote(scale_out.at[j], scale_in.at[d - 1, j], scale_send.at[d - 1, j],
                          scale_recv.at[d - 1, j], peer(d))
            copy.start()
            scale_copies[d, j] = copy

    loaded = 0
    early = min(EARLY, nk)
    for k in range(nk):
        logits(k)
        if k + AHEAD >= nk:
            while loaded < (nk if k == nk - 1 else k + AHEAD + 1 - nk):
                embed_copies[loaded].start()
                loaded += 1
        if k == early - 1:
            pl.semaphore_wait(barrier, len(friends))
            for i in range(early):
                ship(i)
                if i > 0:
                    encode(i - 1)
        elif k >= early:
            ship(k)
            encode(k - 1)
    encode(nk - 1)
    send_scales(0)
    for j in range(1, steps):
        send_codes(j, None)
        send_scales(j)
    q_load(0).start()
    if (2 if steps > 1 else 1) * nt > 1:
        q_load(1).start()

    stat_copies, pair_copies, mix_copies, soft_copies, qp_copies, qx_copies = {}, {}, {}, {}, {}, {}

    def half_of(j):
        return pl.ds(pl.multiple_of(core * hb, hb), hb)

    def softmax(j):
        mine = slice(j * hb, (j + 1) * hb)
        for d in range(1, nx):
            if j > 0:
                code_copies[d, j, None].wait_recv()
            scale_copies[d, j].wait_recv()
        top = None
        for k, (start, size) in enumerate(p.chunks):
            span = slice(start, start + size)
            upper, lower = part[mine, span][:hp], part[mine, span][hp:]
            for d in range(1, nx):
                if j == 0:
                    code_copies[d, j, k].wait_recv()
                word = code_in[d - 1, j, :, span]
                low = scale_in[d - 1, j][:, 2 * k : 2 * k + 1]
                step = scale_in[d - 1, j][:, 2 * k + 1 : 2 * k + 2]
                upper = upper + ((word & 65535).astype(jnp.float32) * step[:hp] + low[:hp])
                lower = lower + (((word >> 16) & 65535).astype(jnp.float32) * step[hp:] + low[hp:])
            part[j * hb : j * hb + hp, span] = upper
            part[j * hb + hp : (j + 1) * hb, span] = lower
            highest = jnp.concatenate(
                [jnp.max(upper, axis=1, keepdims=True), jnp.max(lower, axis=1, keepdims=True)], axis=0)
            top = highest if top is None else jnp.maximum(top, highest)
        total = jnp.zeros_like(top)
        for start, size in p.chunks:
            span = slice(start, start + size)
            e = jnp.exp(part[mine, span] - top)
            weights[j, half_of(j), span] = e.astype(weights.dtype)
            total = total + jnp.sum(e, axis=1, keepdims=True)
        stats[j, z, half_of(j), :] = jnp.where(lane < 64, top, total)
        block_rows = weights.at[j, half_of(j), :]
        copy = remote(block_rows, block_rows, pair_send.at[j], pair_recv.at[j], partner)
        copy.start()
        pair_copies[j] = copy
        for d in range(nz):
            for r in range(2):
                if d == 0 and r == 0:
                    continue
                target = {"req": mate} if r else {}
                if d:
                    target["vocab"] = z_at(d)
                rowset = stats.at[j, z, half_of(j), :]
                copy = remote(rowset, rowset, stat_send.at[j, d, r], stat_recv.at[j, d, r], target)
                copy.start()
                stat_copies[j, d, r] = copy

    half = width // p.halves
    tile = min(512, half)

    def piece_of(j, owner):
        return pl.ds(pl.multiple_of(j * block + owner * piece, piece), piece)

    factors = {}

    def factor_of(j):
        pair_copies[j].wait_recv()
        for d in range(nz):
            for r in range(2):
                if d or r:
                    stat_copies[j, d, r].wait_recv()
        row_top = stats[j, 0][:, 0:1]
        for i in range(1, nz):
            row_top = jnp.maximum(row_top, stats[j, i][:, 0:1])
        row_total = jnp.zeros_like(row_top)
        for i in range(nz):
            other = stats[j, i]
            row_total = row_total + other[:, 64:65] * jnp.exp(other[:, 0:1] - row_top)
        return jnp.exp(stats[j, z][:, 0:1] - row_top) / row_total * act_block[j][:, 0:1]

    def mix(j, h):
        if j == 0 and h == 0:
            for copy in embed_copies:
                copy.wait()
        if h == 0:
            factors[j] = factor_of(j)

        @pl.loop(h * half // tile, (h + 1) * half // tile)
        def _(c):
            columns = pl.ds(pl.multiple_of(c * tile, tile), tile)
            mixed[j * block : (j + 1) * block, columns] = (jnp.dot(
                weights[j, :, 0:words], table[:, columns], preferred_element_type=jnp.float32
            ) * factors[j]).astype(mixed.dtype)

        columns = pl.ds(h * half, half)
        for d in range(1, nz):
            copy = remote(mixed.at[piece_of(j, z_at(d)), columns], inbox.at[j, d - 1, :, columns],
                          mix_send.at[j, h, d - 1], mix_recv.at[j, h, d - 1], {"vocab": z_at(d)})
            copy.start()
            mix_copies[j, h, d] = copy

    unit = min(s, piece)

    def collect(j, h):
        columns = pl.ds(h * half, half)
        total = mixed[piece_of(j, z), columns].astype(jnp.float32)
        for d in range(1, nz):
            mix_copies[j, h, d].wait_recv()
            total = total + inbox[j, d - 1, :, columns].astype(jnp.float32)
        total = total.astype(soft_ref.dtype)
        for u in range(piece // unit):
            at = z * piece + u * unit
            slot = lax.div(at, s) * own_rows + j * s + lax.rem(at, s)
            place = soft_ref.at[pl.ds(pl.multiple_of(slot, unit), unit), columns]
            place[...] = total[u * unit : (u + 1) * unit]
            for d in range(1, nz):
                copy = remote(place, place, soft_send.at[j, h, u, d - 1],
                              soft_recv.at[j, h, u, d - 1], {"vocab": z_at(d)})
                copy.start()
                soft_copies[j, h, u, d] = copy

    gain = gain_ref[...].reshape(1, width).astype(jnp.float32)

    passes = 2 if steps > 1 else 1

    def project(blocks, turn):
        for n, j in enumerate(blocks):
            for h in range(p.halves):
                for u in range(piece // unit):
                    for d in range(1, nz):
                        soft_copies[j, h, u, d].wait_recv()
            for side in range(2):
                for c in range(nx):
                    owner = c * 2 + side
                    v = soft_ref[owner * own_rows + j * s : owner * own_rows + (j + 1) * s, :].astype(jnp.float32)
                    square = jnp.sum(v * v, axis=1, keepdims=True)
                    q_all[j, side, c * s : (c + 1) * s, p.columns :] = jnp.broadcast_to(square, (s, 128))
                    at = n * block + side * hb + c * s
                    scaled[at : at + s, :] = (v * gain).astype(scaled.dtype)
        for i in range(nt):
            g = turn * nt + i
            q_load(g).wait()
            res = jnp.dot(scaled[0 : len(blocks) * block, :], qbuf[g % 2], preferred_element_type=jnp.float32)
            span = slice(i * p.qtile, (i + 1) * p.qtile)
            for n, j in enumerate(blocks):
                q_all[j, 0, :, span] = res[n * block : n * block + hb]
                q_all[j, 1, :, span] = res[n * block + hb : (n + 1) * block]
            if g + 2 < passes * nt:
                q_load(g + 2).start()
        for j in blocks:
            copy = remote(q_all.at[j, 1 - core], q_recv.at[j], qp_send.at[j], qp_recv.at[j], partner)
            copy.start()
            qp_copies[j] = copy

    lane_s = lax.broadcasted_iota(jnp.int32, (s, 128), 1)

    def swap(j):
        qp_copies[j].wait_recv()
        for d in range(1, nx):
            at = pl.ds(pl.multiple_of(chip_at(d) * s, s), s)
            v = q_all[j, core, at, :] + q_recv[j, at, :]
            q_out[j, d - 1, :, : p.columns] = v[:, : p.columns].astype(q_out.dtype)
            square = v[:, p.columns :]
            high = square.astype(q_out.dtype).astype(jnp.float32)
            q_out[j, d - 1, :, p.columns :] = jnp.where(lane_s < 64, high, square - high).astype(q_out.dtype)
            copy = remote(q_out.at[j, d - 1], q_in.at[j, d - 1], qx_send.at[j, d - 1],
                          qx_recv.at[j, d - 1], peer(d))
            copy.start()
            qx_copies[j, d] = copy

    def finish(j):
        at = pl.ds(pl.multiple_of(chip * s, s), s)
        v = q_all[j, core, at, :] + q_recv[j, at, :]
        square = v[:, p.columns : p.columns + 1]
        v = v[:, : p.columns]
        for d in range(1, nx):
            qx_copies[j, d].wait_recv()
            v = v + q_in[j, d - 1, :, : p.columns].astype(jnp.float32)
            sent = q_in[j, d - 1, :, p.columns :].astype(jnp.float32)
            square = square + (sent[:, 0:1] + sent[:, 64:65])
        inv_rms = lax.rsqrt(square / (width * 2 * nx) + 1e-05)
        out_ref[j * s : (j + 1) * s, :] = (v * inv_rms).astype(out_ref.dtype)

    last = steps - 1
    for t in range(steps):
        softmax(t)
        mix(t, 0)
        if t >= 1:
            collect(t - 1, 0)
            collect(t - 1, 1)
        mix(t, 1)
    collect(last, 0)
    collect(last, 1)
    before = list(range(last))
    if before:
        project(before, 0)
        for t in before:
            swap(t)
    project([last], passes - 1)
    swap(last)
    for t in range(steps):
        finish(t)

    for k in range(max(0, nk - RING), nk):
        ring_copies[k].wait_send()
    for group in (code_copies, scale_copies, stat_copies, pair_copies, mix_copies, soft_copies, qp_copies,
                  qx_copies):
        for copy in group.values():
            copy.wait_send()


def hand_over(soft_ref, qkv_ref, soft_out, qkv_out):
    soft_out[...] = soft_ref[...]
    qkv_out[...] = qkv_ref[...]


def on_device(nx, nz, last_states, head_weight, embed_table, norm_gain, qkv_weight, active, slot_request):
    rows, width = last_states.shape
    p = Plan(rows, width, head_weight.shape[1], qkv_weight.shape[1], nx, nz)
    steps, s, hb, hp, block, piece = p.steps, p.s, p.hb, p.hp, p.block, p.piece
    words, nk, far = p.words, len(p.chunks), max(nx - 1, 1)
    padded = round_up(words, 128)
    units = piece // min(s, piece)
    dma, vmem, f32, bf16 = pltpu.SemaphoreType.DMA, pltpu.VMEM, jnp.float32, jnp.bfloat16
    anywhere, inside = pl.BlockSpec(memory_space=pl.ANY), pl.BlockSpec(memory_space=pltpu.VMEM)
    soft, qkv = pl.pallas_call(
        functools.partial(kernel_body, p),
        out_shape=(jax.ShapeDtypeStruct((rows, width), bf16), jax.ShapeDtypeStruct((p.own_rows, p.columns), bf16)),
        in_specs=[anywhere, anywhere, anywhere, inside, anywhere, inside, inside],
        out_specs=(inside, inside),
        scratch_shapes=[
            vmem((words, width), bf16),
            vmem((steps * hb, words), f32),
            vmem((RING, steps * hb, p.chunk), f32),
            vmem((RING, steps * hb, p.chunk), f32),
            vmem((steps, hp, padded), jnp.int32),
            vmem((far, steps, hp, padded), jnp.int32),
            vmem((steps, hb, 128), f32),
            vmem((far, steps, hb, 128), f32),
            vmem((steps, block, padded), bf16),
            vmem((steps, nz, block, 128), f32),
            vmem((rows, 128), f32),
            vmem((steps, block, 128), f32),
            vmem((rows, rows), bf16),
            vmem((rows, rows), bf16),
            vmem((rows, width), bf16),
            vmem((steps, nz - 1, piece, width), bf16),
            vmem((max(1, steps - 1) * block, width), bf16),
            vmem((2, width, p.qtile), bf16),
            vmem((steps, 2, hb, p.qwide), f32),
            vmem((steps, hb, p.qwide), f32),
            vmem((steps, far, s, p.qwide), bf16),
            vmem((steps, far, s, p.qwide), bf16),
            dma, dma((nk,)), dma((nk,)), dma((2,)),
            dma((RING,)), dma((RING,)),
            dma((far, nk + steps)), dma((far, nk + steps)),
            dma((far, steps)), dma((far, steps)),
            dma((steps, nz, 2)), dma((steps, nz, 2)),
            dma((steps,)), dma((steps,)),
            dma((steps, p.halves, nz - 1)), dma((steps, p.halves, nz - 1)),
            dma((steps, p.halves, units, nz - 1)), dma((steps, p.halves, units, nz - 1)),
            dma((steps,)), dma((steps,)),
            dma((steps, far)), dma((steps, far)),
        ],
        compiler_params=pltpu.CompilerParams(
            collective_id=0, has_side_effects=True, vmem_limit_bytes=VMEM_LIMIT
        ),
        name="decode_step",
    )(last_states, head_weight.T, embed_table, norm_gain, qkv_weight, active, slot_request)
    return pl.pallas_call(
        hand_over,
        out_shape=(jax.ShapeDtypeStruct(soft.shape, bf16), jax.ShapeDtypeStruct(qkv.shape, bf16)),
        in_specs=[inside, inside],
        out_specs=(inside, inside),
        name="hand_over",
    )(soft, qkv)


def solution(mesh):
    nx, nz = mesh.shape["req"] // 2, mesh.shape["vocab"]
    return jax.shard_map(
        functools.partial(on_device, nx, nz),
        mesh=mesh,
        in_specs=(
            P("groups", "req"),
            P("req", "vocab"),
            P("vocab", "req"),
            P("req"),
            P("req", "vocab"),
            P("groups"),
            P("groups"),
        ),
        out_specs=(P("groups", "req"), P(("groups", "req"), "vocab")),
        check_vma=False,
    )
```

```python
import functools

import jax
import jax.numpy as jnp
from jax import lax
from jax.experimental import pallas as pl
from jax.experimental.pallas import tpu as pltpu
from jax.sharding import PartitionSpec as P

MESH = pl.DeviceIdType.MESH
VMEM_LIMIT = 63 * 1024 * 1024
RING = 4
EARLY = 4
AHEAD = 2
LEVELS = 65535.0


def remote(src, dst, send, recv, target):
    return pltpu.make_async_remote_copy(
        src_ref=src, dst_ref=dst, send_sem=send, recv_sem=recv, device_id=target, device_id_type=MESH
    )


def round_up(n, m):
    return (n + m - 1) // m * m


def column_chunks(words, chunk):
    whole = words // chunk * chunk
    rest = words - whole
    chunks = [(i * chunk, chunk) for i in range(words // chunk)]
    half = chunk // 2
    if rest > half:
        chunks = [(whole + half, rest - half), (whole, half)] + chunks
    elif rest:
        chunks = [(whole, rest)] + chunks
    return chunks


class Plan:
    def __init__(self, rows, width, words, columns, nx, nz):
        self.rows, self.width, self.words, self.columns = rows, width, words, columns
        self.nx, self.nz = nx, nz
        steps = 4
        while steps > 1 and (rows // steps // nz) % 16:
            steps //= 2
        self.steps = steps
        self.own_rows = rows // (2 * nx)
        self.s = self.own_rows // steps
        self.block = 2 * nx * self.s
        self.hb = self.block // 2
        self.hp = self.hb // 2
        self.piece = self.block // nz
        self.chunk = min(768, width)
        self.chunks = column_chunks(words, self.chunk)
        self.halves = 2
        self.qtile = next(t for t in (512, 640, 256, 128) if columns % t == 0)
        self.qwide = columns + 128


def kernel_body(p, states_ref, head_ref, embed_ref, gain_ref, qkv_ref, active_ref, slot_ref,
                soft_ref, out_ref,
                table, part, ring_out, ring_in, code_out, code_in, scale_out, scale_in,
                weights, stats, act_slot, act_block, hot_slot, hot, mixed, inbox, scaled, qbuf,
                q_all, q_recv, q_out, q_in,
                state_sem, head_sem, embed_sem, q_sem, ring_send, ring_recv, code_send, code_recv,
                scale_send, scale_recv, stat_send, stat_recv, pair_send, pair_recv,
                mix_send, mix_recv, soft_send, soft_recv, qp_send, qp_recv, qx_send, qx_recv):
    nx, nz, steps, s, hb, hp = p.nx, p.nz, p.steps, p.s, p.hb, p.hp
    rows, width, words, own_rows, block, piece = p.rows, p.width, p.words, p.own_rows, p.block, p.piece
    me = lax.axis_index("req")
    z = lax.axis_index("vocab")
    chip, core = lax.div(me, 2), lax.rem(me, 2)
    mate = chip * 2 + (1 - core)
    partner = {"req": mate}

    def chip_at(d):
        return lax.rem(chip + d, nx)

    def peer(d):
        return {"req": chip_at(d) * 2 + core}

    def z_at(d):
        return lax.rem(z + d, nz)

    barrier = pltpu.get_barrier_semaphore()
    friends = ([partner] + [peer(d) for d in range(1, nx)]
               + [{"vocab": z_at(d)} for d in range(1, nz)]
               + [{"vocab": z_at(d), "req": mate} for d in range(1, nz)])
    for friend in friends:
        pl.semaphore_signal(barrier, inc=1, device_id=friend, device_id_type=MESH)

    state_copy = pltpu.make_async_copy(states_ref, mixed, state_sem)
    state_copy.start()
    nk = len(p.chunks)

    def words_of(ref, k):
        start, size = p.chunks[k]
        return ref.at[pl.ds(start, size), :]

    head_copies = [pltpu.make_async_copy(words_of(head_ref, k), words_of(table, k), head_sem.at[k]) for k in range(nk)]
    embed_copies = [pltpu.make_async_copy(words_of(embed_ref, k), words_of(table, k), embed_sem.at[k])
                    for k in range(nk)]
    for k in range(min(nk, AHEAD)):
        head_copies[k].start()

    nt = p.columns // p.qtile

    def q_load(g):
        return pltpu.make_async_copy(
            qkv_ref.at[:, pl.ds(g % nt * p.qtile, p.qtile)], qbuf.at[g % 2], q_sem.at[g % 2])

    request = slot_ref[...].reshape(1, rows)
    choose = (lax.broadcasted_iota(jnp.int32, (rows, rows), 0) == request).astype(jnp.float32)
    hot_slot[...] = choose.T.astype(hot_slot.dtype)
    live = jnp.broadcast_to(active_ref[...].reshape(1, rows).astype(jnp.float32), (128, rows))
    act_slot[...] = live.T
    for h in range(2):
        side = core if h == 0 else 1 - core
        for j in range(steps):
            for o in range(nx):
                to = h * (steps * hb) + j * hb + o * s
                at = pl.multiple_of((side * nx + o) * own_rows + j * s, s)
                hot[to : to + s, :] = hot_slot[pl.ds(at, s), :]
    for j in range(steps):
        for o in range(2 * nx):
            act_block[j, o * s : (o + 1) * s, :] = act_slot[o * own_rows + j * s : o * own_rows + (j + 1) * s, :]
    state_copy.wait()
    wide_tile = min(512, width)

    @pl.loop(0, width // wide_tile)
    def _(c):
        columns = pl.ds(pl.multiple_of(c * wide_tile, wide_tile), wide_tile)
        soft_ref[:, columns] = jnp.dot(
            hot[...], mixed[:, columns], preferred_element_type=jnp.float32
        ).astype(soft_ref.dtype)

    half_rows = steps * hb
    ring_copies, code_copies, scale_copies = {}, {}, {}
    lane = lax.broadcasted_iota(jnp.int32, (hb, 128), 1)

    def logits(k):
        start, size = p.chunks[k]
        slot = k % RING
        head_copies[k].wait()
        if k + AHEAD < nk:
            head_copies[k + AHEAD].start()
        if k >= RING:
            ring_copies[k - RING].wait_send()

        def tile(at, count):
            res = lax.dot_general(soft_ref[...], table[pl.ds(start + at, count), :], (((1,), (1,)), ((), ())),
                                  preferred_element_type=jnp.float32)
            part[:, pl.ds(start + at, count)] = res[:half_rows]
            ring_out[slot, :, pl.ds(at, count)] = res[half_rows:]

        tile(0, size)

    def ship(k):
        size, slot = p.chunks[k][1], k % RING
        span = pl.ds(0, round_up(size, 128))
        copy = remote(ring_out.at[slot, :, span], ring_in.at[slot, :, span],
                      ring_send.at[slot], ring_recv.at[slot], partner)
        copy.start()
        ring_copies[k] = copy

    def encode(k):
        start, size = p.chunks[k]
        slot = k % RING
        ring_copies[k].wait_recv()
        for j in range(steps):
            mine = slice(j * hb, (j + 1) * hb)
            v = part[mine, start : start + size] + ring_in[slot, mine, 0:size]
            part[mine, start : start + size] = v
            low = jnp.min(v, axis=1, keepdims=True)
            step = jnp.maximum((jnp.max(v, axis=1, keepdims=True) - low) / LEVELS, 1e-30)
            level = ((v - low) * (1.0 / step) + 0.5).astype(jnp.int32)
            code_out[j, :, start : start + size] = level[:hp] | (level[hp:] << 16)
            pair = jnp.where(lane == 2 * k, low, step)
            scale_out[j] = pair if k == 0 else jnp.where(lane < 2 * k, scale_out[j], pair)
            if j == 0:
                send_codes(0, k)

    def send_codes(j, k):
        start, size = (0, words) if k is None else p.chunks[k]
        size = round_up(size, 128)
        index = nk + j if k is None else k
        span = pl.ds(start, size)
        for d in range(1, nx):
            copy = remote(code_out.at[j, :, span], code_in.at[d - 1, j, :, span],
                          code_send.at[d - 1, index], code_recv.at[d - 1, index], peer(d))
            copy.start()
            code_copies[d, j, k] = copy

    def send_scales(j):
        for d in range(1, nx):
            copy = remote(scale_out.at[j], scale_in.at[d - 1, j], scale_send.at[d - 1, j],
                          scale_recv.at[d - 1, j], peer(d))
            copy.start()
            scale_copies[d, j] = copy

    loaded = 0
    early = min(EARLY, nk)
    for k in range(nk):
        logits(k)
        if k + AHEAD >= nk:
            while loaded < (nk if k == nk - 1 else k + AHEAD + 1 - nk):
                embed_copies[loaded].start()
                loaded += 1
        if k == early - 1:
            pl.semaphore_wait(barrier, len(friends))
            for i in range(early):
                ship(i)
                if i > 0:
                    encode(i - 1)
        elif k >= early:
            ship(k)
            encode(k - 1)
    encode(nk - 1)
    send_scales(0)
    for j in range(1, steps):
        send_codes(j, None)
        send_scales(j)
    q_load(0).start()
    if (2 if steps > 1 else 1) * nt > 1:
        q_load(1).start()

    stat_copies, pair_copies, mix_copies, soft_copies, qp_copies, qx_copies = {}, {}, {}, {}, {}, {}

    def half_of(j):
        return pl.ds(pl.multiple_of(core * hb, hb), hb)

    def softmax(j):
        mine = slice(j * hb, (j + 1) * hb)
        for d in range(1, nx):
            if j > 0:
                code_copies[d, j, None].wait_recv()
            scale_copies[d, j].wait_recv()
        top = None
        for k, (start, size) in enumerate(p.chunks):
            span = slice(start, start + size)
            upper, lower = part[mine, span][:hp], part[mine, span][hp:]
            for d in range(1, nx):
                if j == 0:
                    code_copies[d, j, k].wait_recv()
                word = code_in[d - 1, j, :, span]
                low = scale_in[d - 1, j][:, 2 * k : 2 * k + 1]
                step = scale_in[d - 1, j][:, 2 * k + 1 : 2 * k + 2]
                upper = upper + ((word & 65535).astype(jnp.float32) * step[:hp] + low[:hp])
                lower = lower + (((word >> 16) & 65535).astype(jnp.float32) * step[hp:] + low[hp:])
            part[j * hb : j * hb + hp, span] = upper
            part[j * hb + hp : (j + 1) * hb, span] = lower
            highest = jnp.concatenate(
                [jnp.max(upper, axis=1, keepdims=True), jnp.max(lower, axis=1, keepdims=True)], axis=0)
            top = highest if top is None else jnp.maximum(top, highest)
        total = jnp.zeros_like(top)
        for start, size in p.chunks:
            span = slice(start, start + size)
            e = jnp.exp(part[mine, span] - top)
            weights[j, half_of(j), span] = e.astype(weights.dtype)
            total = total + jnp.sum(e, axis=1, keepdims=True)
        stats[j, z, half_of(j), :] = jnp.where(lane < 64, top, total)
        block_rows = weights.at[j, half_of(j), :]
        copy = remote(block_rows, block_rows, pair_send.at[j], pair_recv.at[j], partner)
        copy.start()
        pair_copies[j] = copy
        for d in range(nz):
            for r in range(2):
                if d == 0 and r == 0:
                    continue
                target = {"req": mate} if r else {}
                if d:
                    target["vocab"] = z_at(d)
                rowset = stats.at[j, z, half_of(j), :]
                copy = remote(rowset, rowset, stat_send.at[j, d, r], stat_recv.at[j, d, r], target)
                copy.start()
                stat_copies[j, d, r] = copy

    half = width // p.halves
    tile = min(512, half)

    def piece_of(j, owner):
        return pl.ds(pl.multiple_of(j * block + owner * piece, piece), piece)

    factors = {}

    def factor_of(j):
        pair_copies[j].wait_recv()
        for d in range(nz):
            for r in range(2):
                if d or r:
                    stat_copies[j, d, r].wait_recv()
        row_top = stats[j, 0][:, 0:1]
        for i in range(1, nz):
            row_top = jnp.maximum(row_top, stats[j, i][:, 0:1])
        row_total = jnp.zeros_like(row_top)
        for i in range(nz):
            other = stats[j, i]
            row_total = row_total + other[:, 64:65] * jnp.exp(other[:, 0:1] - row_top)
        return jnp.exp(stats[j, z][:, 0:1] - row_top) / row_total * act_block[j][:, 0:1]

    def mix(j, h):
        if j == 0 and h == 0:
            for copy in embed_copies:
                copy.wait()
        if h == 0:
            factors[j] = factor_of(j)

        @pl.loop(h * half // tile, (h + 1) * half // tile)
        def _(c):
            columns = pl.ds(pl.multiple_of(c * tile, tile), tile)
            mixed[j * block : (j + 1) * block, columns] = (jnp.dot(
                weights[j, :, 0:words], table[:, columns], preferred_element_type=jnp.float32
            ) * factors[j]).astype(mixed.dtype)

        columns = pl.ds(h * half, half)
        for d in range(1, nz):
            copy = remote(mixed.at[piece_of(j, z_at(d)), columns], inbox.at[j, d - 1, :, columns],
                          mix_send.at[j, h, d - 1], mix_recv.at[j, h, d - 1], {"vocab": z_at(d)})
            copy.start()
            mix_copies[j, h, d] = copy

    unit = min(s, piece)

    def collect(j, h):
        columns = pl.ds(h * half, half)
        total = mixed[piece_of(j, z), columns].astype(jnp.float32)
        for d in range(1, nz):
            mix_copies[j, h, d].wait_recv()
            total = total + inbox[j, d - 1, :, columns].astype(jnp.float32)
        total = total.astype(soft_ref.dtype)
        for u in range(piece // unit):
            at = z * piece + u * unit
            slot = lax.div(at, s) * own_rows + j * s + lax.rem(at, s)
            place = soft_ref.at[pl.ds(pl.multiple_of(slot, unit), unit), columns]
            place[...] = total[u * unit : (u + 1) * unit]
            for d in range(1, nz):
                copy = remote(place, place, soft_send.at[j, h, u, d - 1],
                              soft_recv.at[j, h, u, d - 1], {"vocab": z_at(d)})
                copy.start()
                soft_copies[j, h, u, d] = copy

    gain = gain_ref[...].reshape(1, width).astype(jnp.float32)

    passes = 2 if steps > 1 else 1

    def project(blocks, turn):
        for n, j in enumerate(blocks):
            for h in range(p.halves):
                for u in range(piece // unit):
                    for d in range(1, nz):
                        soft_copies[j, h, u, d].wait_recv()
            for side in range(2):
                for c in range(nx):
                    owner = c * 2 + side
                    v = soft_ref[owner * own_rows + j * s : owner * own_rows + (j + 1) * s, :].astype(jnp.float32)
                    square = jnp.sum(v * v, axis=1, keepdims=True)
                    q_all[j, side, c * s : (c + 1) * s, p.columns :] = jnp.broadcast_to(square, (s, 128))
                    at = n * block + side * hb + c * s
                    scaled[at : at + s, :] = (v * gain).astype(scaled.dtype)
        for i in range(nt):
            g = turn * nt + i
            q_load(g).wait()
            res = jnp.dot(scaled[0 : len(blocks) * block, :], qbuf[g % 2], preferred_element_type=jnp.float32)
            span = slice(i * p.qtile, (i + 1) * p.qtile)
            for n, j in enumerate(blocks):
                q_all[j, 0, :, span] = res[n * block : n * block + hb]
                q_all[j, 1, :, span] = res[n * block + hb : (n + 1) * block]
            if g + 2 < passes * nt:
                q_load(g + 2).start()
        for j in blocks:
            copy = remote(q_all.at[j, 1 - core], q_recv.at[j], qp_send.at[j], qp_recv.at[j], partner)
            copy.start()
            qp_copies[j] = copy

    lane_s = lax.broadcasted_iota(jnp.int32, (s, 128), 1)

    def swap(j):
        qp_copies[j].wait_recv()
        for d in range(1, nx):
            at = pl.ds(pl.multiple_of(chip_at(d) * s, s), s)
            v = q_all[j, core, at, :] + q_recv[j, at, :]
            q_out[j, d - 1, :, : p.columns] = v[:, : p.columns].astype(q_out.dtype)
            square = v[:, p.columns :]
            high = square.astype(q_out.dtype).astype(jnp.float32)
            q_out[j, d - 1, :, p.columns :] = jnp.where(lane_s < 64, high, square - high).astype(q_out.dtype)
            copy = remote(q_out.at[j, d - 1], q_in.at[j, d - 1], qx_send.at[j, d - 1],
                          qx_recv.at[j, d - 1], peer(d))
            copy.start()
            qx_copies[j, d] = copy

    def finish(j):
        at = pl.ds(pl.multiple_of(chip * s, s), s)
        v = q_all[j, core, at, :] + q_recv[j, at, :]
        square = v[:, p.columns : p.columns + 1]
        v = v[:, : p.columns]
        for d in range(1, nx):
            qx_copies[j, d].wait_recv()
            v = v + q_in[j, d - 1, :, : p.columns].astype(jnp.float32)
            sent = q_in[j, d - 1, :, p.columns :].astype(jnp.float32)
            square = square + (sent[:, 0:1] + sent[:, 64:65])
        inv_rms = lax.rsqrt(square / (width * 2 * nx) + 1e-05)
        out_ref[j * s : (j + 1) * s, :] = (v * inv_rms).astype(out_ref.dtype)

    last = steps - 1
    for t in range(steps):
        softmax(t)
        if t >= 1:
            collect(t - 1, 0)
            collect(t - 1, 1)
        mix(t, 0)
        mix(t, 1)
    collect(last, 0)
    collect(last, 1)
    before = list(range(last))
    if before:
        project(before, 0)
        for t in before:
            swap(t)
    project([last], passes - 1)
    swap(last)
    for t in range(steps):
        finish(t)

    for k in range(max(0, nk - RING), nk):
        ring_copies[k].wait_send()
    for group in (code_copies, scale_copies, stat_copies, pair_copies, mix_copies, soft_copies, qp_copies,
                  qx_copies):
        for copy in group.values():
            copy.wait_send()


def hand_over(soft_ref, qkv_ref, soft_out, qkv_out):
    soft_out[...] = soft_ref[...]
    qkv_out[...] = qkv_ref[...]


def on_device(nx, nz, last_states, head_weight, embed_table, norm_gain, qkv_weight, active, slot_request):
    rows, width = last_states.shape
    p = Plan(rows, width, head_weight.shape[1], qkv_weight.shape[1], nx, nz)
    steps, s, hb, hp, block, piece = p.steps, p.s, p.hb, p.hp, p.block, p.piece
    words, nk, far = p.words, len(p.chunks), max(nx - 1, 1)
    padded = round_up(words, 128)
    units = piece // min(s, piece)
    dma, vmem, f32, bf16 = pltpu.SemaphoreType.DMA, pltpu.VMEM, jnp.float32, jnp.bfloat16
    anywhere, inside = pl.BlockSpec(memory_space=pl.ANY), pl.BlockSpec(memory_space=pltpu.VMEM)
    soft, qkv = pl.pallas_call(
        functools.partial(kernel_body, p),
        out_shape=(jax.ShapeDtypeStruct((rows, width), bf16), jax.ShapeDtypeStruct((p.own_rows, p.columns), bf16)),
        in_specs=[anywhere, anywhere, anywhere, inside, anywhere, inside, inside],
        out_specs=(inside, inside),
        scratch_shapes=[
            vmem((words, width), bf16),
            vmem((steps * hb, words), f32),
            vmem((RING, steps * hb, p.chunk), f32),
            vmem((RING, steps * hb, p.chunk), f32),
            vmem((steps, hp, padded), jnp.int32),
            vmem((far, steps, hp, padded), jnp.int32),
            vmem((steps, hb, 128), f32),
            vmem((far, steps, hb, 128), f32),
            vmem((steps, block, padded), bf16),
            vmem((steps, nz, block, 128), f32),
            vmem((rows, 128), f32),
            vmem((steps, block, 128), f32),
            vmem((rows, rows), bf16),
            vmem((rows, rows), bf16),
            vmem((rows, width), bf16),
            vmem((steps, nz - 1, piece, width), bf16),
            vmem((max(1, steps - 1) * block, width), bf16),
            vmem((2, width, p.qtile), bf16),
            vmem((steps, 2, hb, p.qwide), f32),
            vmem((steps, hb, p.qwide), f32),
            vmem((steps, far, s, p.qwide), bf16),
            vmem((steps, far, s, p.qwide), bf16),
            dma, dma((nk,)), dma((nk,)), dma((2,)),
            dma((RING,)), dma((RING,)),
            dma((far, nk + steps)), dma((far, nk + steps)),
            dma((far, steps)), dma((far, steps)),
            dma((steps, nz, 2)), dma((steps, nz, 2)),
            dma((steps,)), dma((steps,)),
            dma((steps, p.halves, nz - 1)), dma((steps, p.halves, nz - 1)),
            dma((steps, p.halves, units, nz - 1)), dma((steps, p.halves, units, nz - 1)),
            dma((steps,)), dma((steps,)),
            dma((steps, far)), dma((steps, far)),
        ],
        compiler_params=pltpu.CompilerParams(
            collective_id=0, has_side_effects=True, vmem_limit_bytes=VMEM_LIMIT
        ),
        name="decode_step",
    )(last_states, head_weight.T, embed_table, norm_gain, qkv_weight, active, slot_request)
    return pl.pallas_call(
        hand_over,
        out_shape=(jax.ShapeDtypeStruct(soft.shape, bf16), jax.ShapeDtypeStruct(qkv.shape, bf16)),
        in_specs=[inside, inside],
        out_specs=(inside, inside),
        name="hand_over",
    )(soft, qkv)


def solution(mesh):
    nx, nz = mesh.shape["req"] // 2, mesh.shape["vocab"]
    return jax.shard_map(
        functools.partial(on_device, nx, nz),
        mesh=mesh,
        in_specs=(
            P("groups", "req"),
            P("req", "vocab"),
            P("vocab", "req"),
            P("req"),
            P("req", "vocab"),
            P("groups"),
            P("groups"),
        ),
        out_specs=(P("groups", "req"), P(("groups", "req"), "vocab")),
        check_vma=False,
    )
```
